32 devices in a mesh: mode: 16 (over z, x, core), mesh: 2 (over y).
Axes of the slice: x: 2, y: 2, z: 4, core: 2. Of those that a mesh axis runs over, the one named last changes fastest.
Arguments:
- velocity: float32 [3, 11, 11, 2, 32, 512], P(None, None, None, 'mesh', 'mode'), may hold values from -6 to 6
- penalty: float32 [11, 11, 2, 32], P(None, None, 'mesh'), may hold values from 0.5 to 8
Outputs:
- solution: float32 [512, 3, 11, 11, 2, 32], P('mode', None, None, None, 'mesh')
The draws below stay inside these ranges and needn't reach their ends.
All inputs are finite; a program needn't handle non-finite values.
Results may differ from the reference program's by a relative error of at most 0.0001.
Values sent between devices are 32-bit elements; how exact they have to be, the bound alone decides.
No kernel may reach another device: no remote copies, remote signals or barrier semaphores. Data moves between devices by JAX's collectives and lax.ppermute only.
A program may use at most 256 MiB of HBM per device.

```python
import math
import jax
import jax.numpy as jnp
import numpy as np
from jax import lax

ORDER = 10
NQ = 11
PLANES = 512
MODES = 256
ITERS = 6
GX = 2
GY = 32


def block_scale(stream_key, shape, shards, low, high):
    gain = 1.0
    for position, shards_of in shards:
        draws = jax.random.uniform(jax.random.fold_in(jax.random.fold_in(stream_key, 6), position), (shards_of,), jnp.float32, low / len(shards), high / len(shards))
        gain = gain * jnp.repeat(jnp.exp(draws), shape[position] // shards_of).reshape((-1,) + (1,) * (len(shape) - 1 - position))
    return gain


def gaussian(key, dims, spread, reach, pieces=(), kind=jnp.bfloat16):
    factor_of = block_scale(key, dims, pieces, -0.22, 0.18) if pieces else 1.0
    drawn = jax.random.normal(key, dims, jnp.float32) * spread * factor_of
    return jnp.minimum(jnp.maximum(drawn, -reach), reach).astype(kind)


def setup_inputs(seed: int = 0) -> dict:
    streams_of = jax.random.split(jax.random.key(seed), 3)
    velocity = gaussian(streams_of[0], (3, NQ, NQ, GX, GY, PLANES), 1.0, 6.0, ((3, 2), (4, 16)), jnp.float32)
    penalty = jnp.clip(jnp.exp(math.log(8.0) - 2.7725887 * jax.random.uniform(streams_of[1], (NQ, NQ, GX, GY), jnp.float32) ** block_scale(streams_of[1], (NQ, NQ, GX, GY), ((2, 2),), -0.2, 0.2)), 0.5, 8.0)
    return dict(velocity=velocity, penalty=penalty)


helm_base = 1.0
span_wave = 0.02
bound_ratio = 25.0

def legendre_pair(points, order):
    previous = points * 0.0 + 1.0
    current = points * 1.0
    for degree in range(2, order + 1):
        following = ((2 * degree - 1) * points * current - (degree - 1) * previous) / degree
        previous = current
        current = following
    return (current, previous)

def gll_tables(order):
    count = order + 1
    points = -np.cos(np.pi * np.arange(count) / order)
    for sweep in range(200):
        top_vals, below_vals = legendre_pair(points, order)
        points = points - (points * top_vals - below_vals) / (count * top_vals)
    legendre_vals, below_vals = legendre_pair(points, order)
    weights = 2.0 / (order * (order + 1) * legendre_vals ** 2)
    identity = np.eye(count)
    spacing = points[:, None] - points[None, :] + identity
    derivative = legendre_vals[:, None] / (legendre_vals[None, :] * spacing) * (1.0 - identity)
    corner = np.concatenate([[-order * (order + 1) / 4.0], np.zeros(order - 1), [order * (order + 1) / 4.0]])
    derivative = derivative + identity * corner[None, :]
    stiffness = derivative.T @ (weights[:, None] * derivative)
    weight_mat = identity * weights[None, :]
    laplace = np.kron(stiffness, weight_mat) + np.kron(weight_mat, stiffness)
    upper_bound = float(np.max(np.sum(np.abs(laplace), axis=1) / np.sum(laplace * np.eye(count * count), axis=1)))
    weight_vec = jnp.asarray(weights, jnp.float32)
    stiff_mat = jnp.asarray(stiffness, jnp.float32)
    deriv_mat = jnp.asarray(derivative, jnp.float32)
    mass_two = weight_vec[:, None] * weight_vec[None, :]
    stiff_diag = jnp.diagonal(stiff_mat)
    lap_diag = stiff_diag[:, None] * weight_vec[None, :] + weight_vec[:, None] * stiff_diag[None, :]
    return (weight_vec, stiff_mat, deriv_mat, mass_two, lap_diag, upper_bound)

def advect(along_first, along_second, field, deriv_mat):
    grad_first = jnp.einsum('ia,...abxyz->...ibxyz', deriv_mat, field, precision=lax.Precision.HIGHEST)
    grad_second = jnp.einsum('jb,...abxyz->...ajxyz', deriv_mat, field, precision=lax.Precision.HIGHEST)
    return field - (along_first * grad_first + along_second * grad_second)

def make_coeff(first_row, count, penalty, mass_two):
    rows = (first_row + jnp.arange(count, dtype=jnp.int32)).astype(jnp.int32)
    wave = (rows % MODES).astype(jnp.float32)
    helm = helm_base + (span_wave * wave) ** 2
    return (helm[:, None, None, None, None, None] + penalty[None, None]) * mass_two[None, None, :, :, None, None]

def assemble(field, neighbours):
    top = field[:, :, :, -1]
    bottom = field[:, :, :, 0]
    shared = top[..., :-1] + bottom[..., 1:]
    top_new = jnp.concatenate([shared, top[..., -1:]], axis=-1)
    bottom_new = jnp.concatenate([bottom[..., :1], shared], axis=-1)
    field = field.at[:, :, :, -1].set(top_new).at[:, :, :, 0].set(bottom_new)
    right = field[:, :, -1]
    left = field[:, :, 0]
    shared = right[:, :, :, :-1] + left[:, :, :, 1:]
    from_lower, from_upper = neighbours(right[:, :, :, -1], left[:, :, :, 0])
    right_new = jnp.concatenate([shared, (right[:, :, :, -1] + from_upper)[:, :, :, None]], axis=3)
    left_new = jnp.concatenate([(left[:, :, :, 0] + from_lower)[:, :, :, None], shared], axis=3)
    return field.at[:, :, -1].set(right_new).at[:, :, 0].set(left_new)

def no_neighbours(right_edge, left_edge):
    return (jnp.zeros_like(right_edge), jnp.zeros_like(left_edge))

def helm_apply(field, coeff, stiff_mat, weight_vec):
    along_first = jnp.einsum('ia,rcabxy->rcibxy', stiff_mat, field, precision=lax.Precision.HIGHEST)
    along_second = jnp.einsum('jb,rcabxy->rcajxy', stiff_mat, field, precision=lax.Precision.HIGHEST)
    along_first = along_first * weight_vec[None, None, None, :, None, None]
    along_second = along_second * weight_vec[None, None, :, None, None, None]
    return along_first + along_second + coeff * field

def chebyshev(spectra, coeff, tables, neighbours):
    weight_vec, stiff_mat, deriv_mat, mass_two, lap_diag, upper_bound = tables
    lower_bound = upper_bound / bound_ratio
    midpoint = (upper_bound + lower_bound) / 2.0
    half_width = (upper_bound - lower_bound) / 2.0
    rhs = assemble(mass_two[None, None, :, :, None, None] * spectra, neighbours)
    diagonal = assemble(lap_diag[None, None, :, :, None, None] + coeff, neighbours)
    inverse = 1.0 / diagonal
    iterate = jnp.zeros_like(rhs)
    residual = rhs
    direction = inverse * residual / midpoint
    recurrence = half_width / midpoint
    for step in range(ITERS):
        iterate = iterate + direction
        residual = residual - assemble(helm_apply(direction, coeff, stiff_mat, weight_vec), neighbours)
        if step + 1 < ITERS:
            recurrence_next = 1.0 / (2.0 * midpoint / half_width - recurrence)
            direction = recurrence_next * recurrence * direction + 2.0 * recurrence_next / half_width * inverse * residual
            recurrence = recurrence_next
    return iterate

def reference(velocity, penalty):
    tables = gll_tables(ORDER)
    coeff = make_coeff(0, PLANES, penalty, tables[3])
    results = []
    for component in range(3):
        forcing = advect(velocity[0], velocity[1], velocity[component], tables[2])
        transformed = jnp.fft.rfft(forcing, axis=-1)[..., :MODES]
        spectra = jnp.concatenate([jnp.real(transformed), jnp.imag(transformed)], axis=-1) / math.sqrt(PLANES)
        spectra = jnp.moveaxis(spectra, -1, 0)[:, None].astype(jnp.float32)
        results.append(chebyshev(spectra, coeff, tables, no_neighbours))
    return jnp.concatenate(results, axis=1)
```

```python
import functools
import math

import jax
import jax.numpy as jnp
import numpy as np
from jax import lax
from jax.experimental import pallas as pl
from jax.experimental.pallas import tpu as pltpu
from jax.sharding import PartitionSpec as P

MODES = 256
ITERS = 6
LANES = 128
CHUNKS = ((0, 1), (2,))

helm_base = 1.0
span_wave = 0.02
bound_ratio = 25.0


def legendre_pair(points, order):
    previous = points * 0.0 + 1.0
    current = points * 1.0
    for degree in range(2, order + 1):
        following = ((2 * degree - 1) * points * current - (degree - 1) * previous) / degree
        previous = current
        current = following
    return (current, previous)


def gll_tables(order):
    count = order + 1
    points = -np.cos(np.pi * np.arange(count) / order)
    for sweep in range(200):
        top_vals, below_vals = legendre_pair(points, order)
        points = points - (points * top_vals - below_vals) / (count * top_vals)
    legendre_vals, below_vals = legendre_pair(points, order)
    weights = 2.0 / (order * (order + 1) * legendre_vals**2)
    identity = np.eye(count)
    spacing = points[:, None] - points[None, :] + identity
    derivative = legendre_vals[:, None] / (legendre_vals[None, :] * spacing) * (1.0 - identity)
    corner = np.concatenate(
        [[-order * (order + 1) / 4.0], np.zeros(order - 1), [order * (order + 1) / 4.0]]
    )
    derivative = derivative + identity * corner[None, :]
    stiffness = derivative.T @ (weights[:, None] * derivative)
    weight_mat = identity * weights[None, :]
    laplace = np.kron(stiffness, weight_mat) + np.kron(weight_mat, stiffness)
    lap_diag = np.diagonal(laplace)
    upper_bound = float(np.max(np.sum(np.abs(laplace), axis=1) / lap_diag))
    return (weights, derivative, laplace, lap_diag, upper_bound)


def split_table(table):
    table = np.asarray(table, np.float64)
    high = table.astype(jnp.bfloat16)
    low = (table - high.astype(np.float64)).astype(jnp.bfloat16)
    return (high, low)


def split_value(value):
    high = value.astype(jnp.bfloat16)
    low = (value - high.astype(jnp.float32)).astype(jnp.bfloat16)
    return (high, low)


def dft_table(planes):
    turns = np.arange(planes)[None, :] * np.arange(MODES)[:, None] % planes
    angles = 2.0 * np.pi / planes * turns
    return np.concatenate([np.cos(angles), -np.sin(angles)], axis=0) / math.sqrt(planes)


def padded(table, shape):
    result = np.zeros(shape, np.float64)
    result[tuple(slice(0, n) for n in table.shape)] = table
    return result


def dot(a, b, contract=((1,), (0,))):
    return lax.dot_general(a, b, (contract, ((), ())), preferred_element_type=jnp.float32)


def front_kernel(first, second, field, grad_hi, grad_cat, mass, dft_hi, dft_lo, out):
    local, rows, planes = field.shape[1:]
    forcing = []
    for e in range(local):
        value = field[0, e]
        high, low = split_value(value)
        grad = dot(grad_cat[...], jnp.concatenate([high, high], axis=0)) + dot(grad_hi[...], low)
        forcing.append((value - (first[0, e] * grad[:rows] + second[0, e] * grad[rows:])) * mass[...])
    both = ((1,), (1,))
    kept = out.shape[3]
    for start in range(0, local, 2):
        pair = forcing[start : start + 2]
        high, low = split_value(jnp.concatenate(pair, axis=0))
        spectra = (
            dot(dft_hi[...], high, both)
            + dot(dft_hi[...], low, both)
            + dot(dft_lo[...], high, both)
        )
        for i in range(len(pair)):
            part = spectra[:, i * rows : (i + 1) * rows]
            out[:, 0, start + i] = part.reshape(out.shape[0], kept, rows)


def front(planes_first, first, count, tables, peers):
    comps, local, rows, planes = planes_first.shape
    kept = tables[-1].shape[0] // peers

    def pick(index):
        return pl.BlockSpec((1, local, rows, planes), lambda c: (index(c), 0, 0, 0))

    def whole(table):
        return pl.BlockSpec(table.shape, lambda c: (0,) * table.ndim)

    return pl.pallas_call(
        front_kernel,
        out_shape=jax.ShapeDtypeStruct((peers, count, local, kept, rows), jnp.float32),
        grid=(count,),
        in_specs=[pick(lambda c: 0), pick(lambda c: 1), pick(lambda c: c + first)]
        + [whole(t) for t in tables],
        out_specs=pl.BlockSpec((peers, 1, local, kept, rows), lambda c: (0, c, 0, 0, 0)),
        name=f"front{first}",
    )(planes_first, planes_first, planes_first, *tables)


def shared_sums(tiles, masks):
    top, bottom, right, left = masks
    summed = []
    for column in tiles:
        line = []
        for row, value in enumerate(column):
            after = column[row + 1] if row + 1 < len(column) else None
            before = column[row - 1] if row > 0 else None
            extra = 0.0
            if before is not None:
                extra = jnp.where(bottom, pltpu.roll(before, LANES - 10, 1), extra)
            if after is not None:
                extra = jnp.where(top, pltpu.roll(after, 10, 1), extra)
            line.append(value + extra)
        summed.append(line)
    result = []
    for col, line in enumerate(summed):
        values = []
        for row, value in enumerate(line):
            extra = 0.0
            if col > 0:
                extra = jnp.where(left, pltpu.roll(summed[col - 1][row], LANES - 110, 1), extra)
            if col + 1 < len(summed):
                extra = jnp.where(right, pltpu.roll(summed[col + 1][row], 110, 1), extra)
            values.append(value if isinstance(extra, float) else value + extra)
        result.append(values)
    return result


def read_masks(mask_ref):
    return tuple(mask_ref[i] > 0.5 for i in range(4))


def places(shape, kept):
    groups, owners, local_cols, local_rows = shape
    table = []
    for col in range(owners * local_cols):
        owner, lc = divmod(col, local_cols)
        line = []
        for row in range(groups * local_rows):
            part, e = divmod(row, local_rows)
            line.append((((part * owners + owner) * local_cols + lc) * local_rows + e) * kept)
        table.append(line)
    return table


def prep_kernel(shape, wave_ref, pen_ref, lap_ref, mask_ref, inverse_ref):
    masks = read_masks(mask_ref)
    kept = wave_ref.shape[0]
    where = places(shape, kept)
    base = wave_ref[...] + lap_ref[...]
    tiles = [
        [base + pen_ref[col, row : row + 1, :] for row in range(len(where[col]))]
        for col in range(len(where))
    ]
    for line, rows in zip(shared_sums(tiles, masks), where):
        for value, first in zip(line, rows):
            inverse_ref[first : first + kept, :] = 1.0 / value


def solve_kernel(
    shape, midpoint, spot_ref, gain_ref, src_ref, inverse_ref, mat_ref, mask_ref, *rest
):
    groups, owners, local_cols, local_rows = shape
    outs = rest[:-4]
    work_ref, res_ref, dir_ref, sum_ref = rest[-4:]
    masks = read_masks(mask_ref)
    kept = src_ref.shape[-2]
    where = places(shape, kept)
    cols, rows_all = len(where), len(where[0])
    total = cols * rows_all * kept
    block = total // math.gcd(groups, 4)

    def tile(ref, col, row):
        return ref[pl.ds(where[col][row], kept), :]

    def pieces(ref):
        return [[tile(ref, col, row) for row in range(rows_all)] for col in range(cols)]

    def source(col, row):
        owner, lc = divmod(col, local_cols)
        part, e = divmod(row, local_rows)
        return src_ref[part, owner, 0, lc * local_rows + e]

    first = shared_sums(
        [[source(col, row) for row in range(rows_all)] for col in range(cols)], masks
    )
    for col in range(cols):
        for row in range(rows_all):
            here = pl.ds(where[col][row], kept)
            residual = inverse_ref[here, :] * first[col][row]
            direction = residual * (1.0 / midpoint)
            res_ref[here, :] = residual
            dir_ref[here, :] = direction
            sum_ref[pl.ds((col * rows_all + row) * kept, kept), :] = direction

    def sweep(step, carry):
        keep = gain_ref[step, 0]
        gain = gain_ref[step, 1]
        for start in range(0, total, block):
            high, low = split_value(dir_ref[pl.ds(start, block), :])
            product = dot(jnp.concatenate([high, low], axis=1), mat_ref[...])
            work_ref[pl.ds(start, block), :] = product[:, :LANES] + product[:, LANES:]
        summed = shared_sums(pieces(work_ref), masks)
        for col in range(cols):
            for row in range(rows_all):
                here = pl.ds(where[col][row], kept)
                direction = dir_ref[here, :]
                residual = res_ref[here, :] - direction - inverse_ref[here, :] * summed[col][row]
                direction = keep * direction + gain * residual
                res_ref[here, :] = residual
                dir_ref[here, :] = direction
                there = pl.ds((col * rows_all + row) * kept, kept)
                sum_ref[there, :] = sum_ref[there, :] + direction
        return carry

    lax.fori_loop(0, ITERS - 1, sweep, 0)

    spot = spot_ref[0]
    for shift, out in enumerate(outs):
        for lc in range(local_cols):
            col = lax.rem(spot + shift, owners) * local_cols + lc
            for k in range(kept):
                out[k, lc] = sum_ref[pl.ds(col * (rows_all * kept) + k, rows_all, stride=kept), :]


def solve(shape, midpoint, component, slot, spot, gains, moved, inverse, mat, masks):
    groups, owners, local_cols, local_rows = shape
    kept = moved.shape[-2]
    rows = groups * local_rows
    total = owners * local_cols * rows * kept
    piece = jax.ShapeDtypeStruct((kept, local_cols, rows, LANES), jnp.float32)
    smem = pl.BlockSpec(memory_space=pltpu.SMEM)
    vmem = pl.BlockSpec(memory_space=pltpu.VMEM)
    block = moved.shape[:2] + (1,) + moved.shape[3:]
    return pl.pallas_call(
        functools.partial(solve_kernel, shape, midpoint),
        out_shape=[piece] * owners,
        grid=(1,),
        in_specs=[
            smem,
            smem,
            pl.BlockSpec(block, lambda i: (0, 0, slot, 0, 0, 0)),
            vmem,
            vmem,
            vmem,
        ],
        out_specs=[vmem] * owners,
        scratch_shapes=[pltpu.VMEM((total, LANES), jnp.float32)] * 4,
        name=f"solve{component}",
    )(spot, gains, moved, inverse, mat, masks)


def finish_kernel(component, place_ref, src_ref, *rest):
    out_ref, stage_ref, sems = rest[-3:]
    nodes = stage_ref.shape[1]
    kept = src_ref.shape[0]
    copies = []
    for k in range(kept):
        for lc in range(src_ref.shape[1]):
            stage_ref[k, :, lc, :] = src_ref[k, lc].T[:nodes]
        target = out_ref.at[place_ref[0] * kept + k, component]
        copy = pltpu.make_async_copy(stage_ref.at[k], target, sems.at[k])
        copy.start()
        copies.append(copy)
    for copy in copies:
        copy.wait()


def finish(place, component, comps, modes, nodes, source, so_far):
    kept, local_cols, rows, lanes = source.shape
    keep_out = pl.BlockSpec(memory_space=pl.ANY)
    in_specs = [pl.BlockSpec(memory_space=pltpu.SMEM), pl.BlockSpec(memory_space=pltpu.VMEM)]
    args = [place, source]
    aliases = {}
    if so_far is not None:
        in_specs.append(keep_out)
        args.append(so_far)
        aliases = {2: 0}
    return pl.pallas_call(
        functools.partial(finish_kernel, component),
        out_shape=jax.ShapeDtypeStruct((modes, comps, nodes, local_cols, rows), jnp.float32),
        in_specs=in_specs,
        out_specs=keep_out,
        scratch_shapes=[
            pltpu.VMEM((kept, nodes, local_cols, rows), jnp.float32),
            pltpu.SemaphoreType.DMA((kept,)),
        ],
        input_output_aliases=aliases,
        name=f"finish{component}",
    )(*args)


def per_device(velocity, penalty):
    comps, count, _, local_cols, local_rows, planes = velocity.shape
    nodes = count * count
    groups = lax.axis_size("mode")
    owners = lax.axis_size("mesh")
    peers = groups * owners
    spot = lax.axis_index("mesh")
    local = local_cols * local_rows
    kept = 2 * MODES // peers
    total_cols = owners * local_cols
    total_rows = groups * local_rows

    weights, derivative, laplace, lap_diag, upper_bound = gll_tables(count - 1)
    mass = np.kron(weights, weights)
    lower_bound = upper_bound / bound_ratio
    midpoint = (upper_bound + lower_bound) / 2.0
    half_width = (upper_bound - lower_bound) / 2.0
    recurrence = half_width / midpoint
    gains = []
    for step in range(1, ITERS):
        following = 1.0 / (2.0 * midpoint / half_width - recurrence)
        gains.append((following * recurrence, 2.0 * following / half_width))
        recurrence = following
    gains = jnp.asarray(np.array(gains), jnp.float32)
    identity = np.eye(count)
    grads = np.concatenate(
        [
            padded(np.kron(derivative, identity), (LANES, LANES)),
            padded(np.kron(identity, derivative), (LANES, LANES)),
        ]
    )
    grad_hi, grad_lo = split_table(grads)
    dft_hi, dft_lo = split_table(dft_table(planes))
    mass_col = padded(mass[:, None], (LANES, 1)).astype(np.float32)
    grad_cat = np.concatenate([grad_hi, grad_lo], axis=1)
    front_tables = [jnp.asarray(t) for t in (grad_hi, grad_cat, mass_col, dft_hi, dft_lo)]
    off_diag = laplace.T - np.diag(lap_diag)
    mat_hi, mat_lo = split_table(padded(off_diag, (LANES, LANES)))
    half = np.concatenate([mat_hi, mat_lo], axis=1)
    mat = jnp.asarray(np.concatenate([half, half], axis=0))
    node = np.arange(LANES)
    real = node < nodes
    masks = np.stack(
        [
            real & (node % count == count - 1),
            real & (node % count == 0),
            real & (node // count == count - 1),
            real & (node // count == 0),
        ]
    ).astype(np.float32)
    masks = jnp.asarray(np.broadcast_to(masks[:, None], (4, kept, LANES)))
    lap_row = np.ones((1, LANES))
    lap_row[0, :nodes] = lap_diag
    lap_row = jnp.asarray(lap_row, jnp.float32)
    mass_row = jnp.asarray(padded(mass[None], (1, LANES)), jnp.float32)

    own = penalty.reshape(nodes, local_cols, total_rows).transpose(1, 2, 0)
    own = jnp.pad(own, ((0, 0), (0, 0), (0, LANES - nodes))) * mass_row
    full = jnp.zeros((total_cols, total_rows, LANES), jnp.float32)
    full = lax.dynamic_update_slice(full, own, (spot * local_cols, 0, 0))
    for shift in range(1, owners):
        ring = [(i, (i + shift) % owners) for i in range(owners)]
        other = lax.ppermute(own, "mesh", ring)
        full = lax.dynamic_update_slice(
            full, other, (lax.rem(spot + owners - shift, owners) * local_cols, 0, 0)
        )
    first_row = (lax.axis_index("mode") * owners + spot) * kept
    wave = ((first_row + jnp.arange(kept, dtype=jnp.int32)) % MODES).astype(jnp.float32)
    helm = helm_base + (span_wave * wave) ** 2
    wave_mass = helm[:, None] * mass_row

    shape = (groups, owners, local_cols, local_rows)
    total = peers * local * kept
    inverse = pl.pallas_call(
        functools.partial(prep_kernel, shape),
        out_shape=jax.ShapeDtypeStruct((total, LANES), jnp.float32),
        name="prep",
    )(wave_mass, full, lap_row, masks)

    planes_first = velocity.reshape(comps, nodes, local, planes).transpose(0, 2, 1, 3)
    planes_first = jnp.pad(planes_first, ((0, 0), (0, 0), (0, LANES - nodes), (0, 0)))

    spot_arg = spot.astype(jnp.int32)[None]
    result = None
    for chunk in CHUNKS:
        spectra = front(planes_first, chunk[0], len(chunk), front_tables, peers)
        moved = lax.all_to_all(spectra, ("mode", "mesh"), split_axis=0, concat_axis=0, tiled=True)
        moved = moved.reshape((groups, owners) + moved.shape[1:])
        for slot, component in enumerate(chunk):
            solved = solve(
                shape, midpoint, component, slot, spot_arg, gains, moved, inverse, mat, masks
            )
            for shift in range(owners):
                part = solved[shift]
                if shift:
                    ring = [(i, (i + shift) % owners) for i in range(owners)]
                    part = lax.ppermute(part, "mesh", ring)
                place = lax.rem(spot_arg + (owners - shift), owners)
                result = finish(place, component, comps, kept * owners, nodes, part, result)
    return result.reshape(kept * owners, comps, count, count, local_cols, total_rows)


def solution(mesh):
    return jax.shard_map(
        per_device,
        mesh=mesh,
        in_specs=(P(None, None, None, "mesh", "mode", None), P(None, None, "mesh", None)),
        out_specs=P("mode", None, None, None, "mesh", None),
        check_vma=False,
    )
```

```python
import functools
import math

import jax
import jax.numpy as jnp
import numpy as np
from jax import lax
from jax.experimental import pallas as pl
from jax.experimental.pallas import tpu as pltpu
from jax.sharding import PartitionSpec as P

MODES = 256
ITERS = 6
LANES = 128
GRANT = 16 << 20
CHUNKS = ((0, 1), (2,))

helm_base = 1.0
span_wave = 0.02
bound_ratio = 25.0


def legendre_pair(points, order):
    previous = points * 0.0 + 1.0
    current = points * 1.0
    for degree in range(2, order + 1):
        following = ((2 * degree - 1) * points * current - (degree - 1) * previous) / degree
        previous = current
        current = following
    return (current, previous)


def gll_tables(order):
    count = order + 1
    points = -np.cos(np.pi * np.arange(count) / order)
    for _ in range(200):
        top_vals, below_vals = legendre_pair(points, order)
        points = points - (points * top_vals - below_vals) / (count * top_vals)
    legendre_vals, below_vals = legendre_pair(points, order)
    weights = 2.0 / (order * (order + 1) * legendre_vals**2)
    identity = np.eye(count)
    spacing = points[:, None] - points[None, :] + identity
    derivative = legendre_vals[:, None] / (legendre_vals[None, :] * spacing) * (1.0 - identity)
    corner = np.concatenate(
        [[-order * (order + 1) / 4.0], np.zeros(order - 1), [order * (order + 1) / 4.0]]
    )
    derivative = derivative + identity * corner[None, :]
    stiffness = derivative.T @ (weights[:, None] * derivative)
    weight_mat = identity * weights[None, :]
    laplace = np.kron(stiffness, weight_mat) + np.kron(weight_mat, stiffness)
    lap_diag = np.diagonal(laplace)
    upper_bound = float(np.max(np.sum(np.abs(laplace), axis=1) / lap_diag))
    return (weights, derivative, laplace, lap_diag, upper_bound)


def split_table(table):
    table = np.asarray(table, np.float64)
    high = table.astype(jnp.bfloat16)
    low = (table - high.astype(np.float64)).astype(jnp.bfloat16)
    return (high, low)


def split_value(value):
    high = value.astype(jnp.bfloat16)
    low = (value - high.astype(jnp.float32)).astype(jnp.bfloat16)
    return (high, low)


def dft_tables(planes, kept, order):
    halves = len(order)
    first = np.arange(0, 2 * MODES, kept)
    tables = []
    for half in range(halves):
        row = (first[:, None] + np.array(order[half])[None, :]).reshape(-1)
        turns = np.arange(planes // halves)[None, :] * (row % MODES)[:, None] % planes
        angles = 2.0 * np.pi / planes * turns
        table = np.where((row < MODES)[:, None], np.cos(angles), -np.sin(angles))
        high, low = split_table(table / math.sqrt(planes))
        tables.append(np.concatenate([high, low], axis=1))
    return np.stack(tables)


def resident(value):
    return pltpu.with_memory_space_constraint(value, pltpu.VMEM)


def remote(value):
    return pltpu.with_memory_space_constraint(value, pltpu.HBM)


def padded(table, shape):
    result = np.zeros(shape, np.float64)
    result[tuple(slice(0, n) for n in table.shape)] = table
    return result


def dot(a, b, contract=((1,), (0,))):
    return lax.dot_general(a, b, (contract, ((), ())), preferred_element_type=jnp.float32)


def front_kernel(
    chunk, halves, local, field_ref, grad_ref, mass, dft_ref, out_ref, stage, grad, dft, ready, sems, out_sems
):
    comps, flat, lanes = field_ref.shape
    _, _, _, kept_all, rows = out_ref.shape
    kept = kept_all // halves
    planes = dft.shape[2] // 2 * halves
    pieces = planes // lanes
    nodes = flat // (pieces * local)
    order = [0, 1] + [c for c in chunk if c > 1]
    copies = {c: pltpu.make_async_copy(field_ref.at[c], stage.at[c], sems.at[c]) for c in order}
    grad_copy = pltpu.make_async_copy(grad_ref, grad, sems.at[comps])
    dft_copy = pltpu.make_async_copy(dft_ref, dft, sems.at[comps + 1])
    copies[0].start()
    grad_copy.start()
    for c in order[1:]:
        copies[c].start()
    dft_copy.start()
    gap = jnp.zeros((rows - nodes, planes), jnp.float32)

    def read(c, e):
        parts = [
            stage[c, pl.ds(piece * local + e, nodes, stride=pieces * local), :]
            for piece in range(pieces)
        ]
        return jnp.concatenate([jnp.concatenate(parts, axis=1), gap], axis=0)

    grad_copy.wait()
    copies[0].wait()
    copies[1].wait()
    for c in order[2:]:
        copies[c].wait()
    sent = []
    for slot, c in enumerate(chunk):
        for start in range(0, local, 2):
            elements = range(start, min(start + 2, local))
            folded = [[] for _ in range(halves)]
            for e in elements:
                value = read(c, e)
                high, low = split_value(value)
                slope = dot(grad[...], jnp.concatenate([high, low, high], axis=0))
                forcing = value - (read(0, e) * slope[:rows] + read(1, e) * slope[rows:])
                if halves == 2:
                    near, far = forcing[:, : planes // 2], forcing[:, planes // 2 :]
                    folded[0].append(near + far)
                    folded[1].append(near - far)
                else:
                    folded[0].append(forcing)
            if slot == 0 and start == 0:
                dft_copy.wait()
            for half in range(halves):
                high, low = split_value(jnp.concatenate(folded[half], axis=0))
                table = dft[half]
                spectra = dot(
                    jnp.concatenate([table[:, : planes // halves], table], axis=1),
                    jnp.concatenate([high, low, high], axis=1),
                    ((1,), (1,)),
                )
                for i, e in enumerate(elements):
                    part = spectra[:, i * rows : (i + 1) * rows] * mass[...]
                    ready[:, slot, e, half * kept : (half + 1) * kept, :] = part.reshape(
                        out_ref.shape[0], kept, rows
                    )
        copy = pltpu.make_async_copy(ready.at[:, slot], out_ref.at[:, slot], out_sems.at[slot])
        copy.start()
        sent.append(copy)
    for copy in sent:
        copy.wait()


def front(field, chunk, halves, local, tables, peers):
    grad, mass, dft = tables
    kept = dft.shape[0] * dft.shape[1] // peers
    far = pl.BlockSpec(memory_space=pltpu.HBM)
    shape = (peers, len(chunk), local, kept, LANES)
    return pl.pallas_call(
        functools.partial(front_kernel, chunk, halves, local),
        out_shape=pltpu.HBM(shape, jnp.float32),
        in_specs=[far, far, pl.BlockSpec(memory_space=pltpu.VMEM), far],
        out_specs=far,
        scratch_shapes=[
            pltpu.VMEM(field.shape, jnp.float32),
            pltpu.VMEM(grad.shape, grad.dtype),
            pltpu.VMEM(dft.shape, dft.dtype),
            pltpu.VMEM(shape, jnp.float32),
            pltpu.SemaphoreType.DMA((field.shape[0] + 2,)),
            pltpu.SemaphoreType.DMA((len(chunk),)),
        ],
        compiler_params=pltpu.CompilerParams(vmem_limit_bytes=GRANT),
    )(remote(field), remote(grad), mass, remote(dft))


def side_sum(value, before, after, masks):
    first, last = masks
    extra = 0.0
    if before is not None:
        extra = jnp.where(first, before, extra)
    if after is not None:
        extra = jnp.where(last, after, extra)
    return value if before is None and after is None else value + extra


def across(line, masks, side):
    result = []
    for col, value in enumerate(line):
        before = pltpu.roll(line[col - 1], LANES - side, 1) if col > 0 else None
        after = pltpu.roll(line[col + 1], side, 1) if col + 1 < len(line) else None
        result.append(side_sum(value, before, after, masks))
    return result


def read_masks(mask_ref, kept):
    bottom, top, left, right = (
        jnp.broadcast_to(mask_ref[i : i + 1, :], (kept, LANES)) > 0.5 for i in range(4)
    )
    return (bottom, top), (left, right)


def places(shape, kept):
    groups, owners, local_cols, local_rows = shape
    table = []
    for col in range(owners * local_cols):
        owner, lc = divmod(col, local_cols)
        line = []
        for row in range(groups * local_rows):
            part, e = divmod(row, local_rows)
            line.append((((part * owners + owner) * local_cols + lc) * local_rows + e) * kept)
        table.append(line)
    return table


def prep_kernel(shape, count, wave_ref, pen_ref, lap_ref, mask_ref, inverse_ref):
    kept = wave_ref.shape[0]
    along, over = read_masks(mask_ref, kept)
    where = places(shape, kept)
    cols, rows = len(where), len(where[0])
    base = wave_ref[...] + lap_ref[...]
    edge = pltpu.roll(base, count - 1, 1), pltpu.roll(base, LANES - count + 1, 1)
    for row in range(rows):
        line = []
        for col in range(cols):
            before = after = None
            if row > 0:
                other = pltpu.roll(pen_ref[col, row - 1 : row, :], LANES - count + 1, 1)
                before = edge[1] + other
            if row + 1 < rows:
                after = edge[0] + pltpu.roll(pen_ref[col, row + 1 : row + 2, :], count - 1, 1)
            line.append(side_sum(base + pen_ref[col, row : row + 1, :], before, after, along))
        for col, value in enumerate(across(line, over, (count - 1) * count)):
            first = where[col][row]
            inverse_ref[first : first + kept, :] = 1.0 / value


def solve_kernel(
    shape, midpoint, side, slot, span, gains, spot_ref, src_ref, inverse_ref, mat_ref, swap_ref, mask_ref, *rest
):
    groups, owners, local_cols, local_rows = shape
    outs = rest[:-5]
    work_ref, edge_ref, res_ref, dir_ref, sum_ref = rest[-5:]
    begin, end = span
    kept = end - begin
    along, over = read_masks(mask_ref, kept)
    where = places(shape, kept)
    whole = places(shape, src_ref.shape[-2])
    cols, rows_all = len(where), len(where[0])
    total = cols * rows_all * kept
    steps = math.gcd(groups, 4)
    block = total // steps
    parts = groups // steps

    def assembled(main, row):
        line = []
        for col in range(cols):
            before = after = None
            if row > 0:
                before = edge_ref[pl.ds(where[col][row - 1], kept), :]
            if row + 1 < rows_all:
                after = edge_ref[pl.ds(where[col][row + 1], kept), :]
            line.append(side_sum(main(col, row), before, after, along))
        return across(line, over, side)

    def source(col, row):
        owner, lc = divmod(col, local_cols)
        part, e = divmod(row, local_rows)
        return src_ref[part, owner, slot, lc * local_rows + e, begin:end]

    def inverse(col, row):
        return inverse_ref[pl.ds(whole[col][row] + begin, kept), :]

    def work(col, row):
        return work_ref[pl.ds(where[col][row], kept), :]

    for step in range(steps):
        values = src_ref[step * parts : (step + 1) * parts, :, slot, :, begin:end]
        values = values.reshape(block, LANES)
        high, low = split_value(values)
        edge_ref[pl.ds(step * block, block), :] = dot(
            jnp.concatenate([high, low], axis=1), swap_ref[...]
        )
    for row in range(rows_all):
        for col, value in enumerate(assembled(source, row)):
            here = pl.ds(where[col][row], kept)
            residual = inverse(col, row) * value
            direction = residual * (1.0 / midpoint)
            res_ref[here, :] = residual
            dir_ref[here, :] = direction
            sum_ref[pl.ds((col * rows_all + row) * kept, kept), :] = direction

    def sweep(step, carry):
        keep, gain = (jnp.float32(value) for value in gains[0])
        for i, (next_keep, next_gain) in enumerate(gains[1:]):
            keep = jnp.where(step > i, jnp.float32(next_keep), keep)
            gain = jnp.where(step > i, jnp.float32(next_gain), gain)

        def multiply(start):
            high, low = split_value(dir_ref[pl.ds(start, block), :])
            product = dot(jnp.concatenate([high, low, high], axis=1), mat_ref[...])
            work_ref[pl.ds(start, block), :] = product[:, :LANES]
            edge_ref[pl.ds(start, block), :] = product[:, LANES:]

        def update(row):
            for col, value in enumerate(assembled(work, row)):
                here = pl.ds(where[col][row], kept)
                direction = dir_ref[here, :]
                residual = res_ref[here, :] - direction - inverse(col, row) * value
                direction = keep * direction + gain * residual
                res_ref[here, :] = residual
                dir_ref[here, :] = direction
                there = pl.ds((col * rows_all + row) * kept, kept)
                sum_ref[there, :] = sum_ref[there, :] + direction

        done = 0
        multiply(0)
        for piece in range(1, steps + 1):
            if piece < steps:
                multiply(piece * block)
            ready = rows_all if piece == steps else piece * parts * local_rows - 1
            for row in range(done, ready):
                update(row)
            done = ready
        return carry

    lax.fori_loop(0, ITERS - 1, sweep, 0)

    spot = spot_ref[0]
    for shift, out in enumerate(outs):
        for lc in range(local_cols):
            col = lax.rem(spot + shift, owners) * local_cols + lc
            for k in range(kept):
                out[k, lc] = sum_ref[pl.ds(col * (rows_all * kept) + k, rows_all, stride=kept), :]


def solve(shape, midpoint, side, slot, span, spot, gains, moved, inverse, mat, swap, masks):
    groups, owners, local_cols, local_rows = shape
    kept = span[1] - span[0]
    rows = groups * local_rows
    total = owners * local_cols * rows * kept
    piece = pltpu.VMEM((kept, local_cols, rows, LANES), jnp.float32)
    smem = pl.BlockSpec(memory_space=pltpu.SMEM)
    vmem = pl.BlockSpec(memory_space=pltpu.VMEM)
    return pl.pallas_call(
        functools.partial(solve_kernel, shape, midpoint, side, slot, span, gains),
        out_shape=[piece] * owners,
        in_specs=[
            smem,
            vmem,
            vmem,
            vmem,
            vmem,
            vmem,
        ],
        out_specs=[vmem] * owners,
        scratch_shapes=[pltpu.VMEM((total, LANES), jnp.float32)] * 5,
        compiler_params=pltpu.CompilerParams(vmem_limit_bytes=GRANT),
    )(spot, *[resident(v) for v in (moved, inverse, mat, swap, masks)])


def finish_kernel(parts, owners, kept, order, spot_ref, *rest):
    sources = rest[: len(parts)]
    out_ref, stage_ref, sems = rest[-3:]
    nodes, local_cols, lanes = stage_ref.shape[1:]
    rows = sources[0].shape[2]
    fit = lanes // rows
    copies = []
    for source, (component, shift, begin) in zip(sources, parts):
        place = lax.rem(spot_ref[0] + (owners - shift), owners) * kept
        count = source.shape[0]
        for first in range(0, count, fit):
            group = range(first, min(first + fit, count))
            for lc in range(local_cols):
                block = [source[k, lc] for k in group]
                if len(group) * rows < lanes:
                    block.append(jnp.zeros((lanes - len(group) * rows, LANES), jnp.float32))
                turned = jnp.concatenate(block, axis=0).T
                for i, k in enumerate(group):
                    value = pltpu.roll(turned, lanes - i * rows, 1) if i else turned
                    stage_ref[len(copies) + i, :, lc, :] = value[:nodes]
            for k in group:
                target = out_ref.at[place + order[begin + k], component]
                index = len(copies)
                copy = pltpu.make_async_copy(stage_ref.at[index], target, sems.at[index])
                copy.start()
                copies.append(copy)
    for copy in copies:
        copy.wait()


def finish(parts, owners, kept, order, comps, nodes, spot, sources, so_far):
    _, local_cols, rows, _ = sources[0].shape
    width = pl.cdiv(rows, LANES) * LANES
    count = sum(source.shape[0] for source in sources)
    keep_out = pl.BlockSpec(memory_space=pl.ANY)
    in_specs = [pl.BlockSpec(memory_space=pltpu.SMEM)]
    in_specs += [pl.BlockSpec(memory_space=pltpu.VMEM)] * len(sources)
    args = [spot] + [resident(source) for source in sources]
    aliases = {}
    if so_far is not None:
        aliases = {len(args): 0}
        in_specs.append(keep_out)
        args.append(so_far)
    return pl.pallas_call(
        functools.partial(finish_kernel, parts, owners, kept, order),
        out_shape=jax.ShapeDtypeStruct((kept * owners, comps, nodes, local_cols, width), jnp.float32),
        in_specs=in_specs,
        out_specs=keep_out,
        scratch_shapes=[
            pltpu.VMEM((count, nodes, local_cols, width), jnp.float32),
            pltpu.SemaphoreType.DMA((count,)),
        ],
        input_output_aliases=aliases,
        compiler_params=pltpu.CompilerParams(vmem_limit_bytes=GRANT),
    )(*args)


def step(velocity, penalty):
    comps, count, _, local_cols, local_rows, planes = velocity.shape
    nodes = count * count
    groups = lax.axis_size("mode")
    owners = lax.axis_size("mesh")
    peers = groups * owners
    spot = lax.axis_index("mesh")
    local = local_cols * local_rows
    kept = 2 * MODES // peers
    total_cols = owners * local_cols
    total_rows = groups * local_rows

    weights, derivative, laplace, lap_diag, upper_bound = gll_tables(count - 1)
    mass = np.kron(weights, weights)
    lower_bound = upper_bound / bound_ratio
    midpoint = (upper_bound + lower_bound) / 2.0
    half_width = (upper_bound - lower_bound) / 2.0
    recurrence = half_width / midpoint
    gains = []
    for _ in range(1, ITERS):
        following = 1.0 / (2.0 * midpoint / half_width - recurrence)
        gains.append((following * recurrence, 2.0 * following / half_width))
        recurrence = following
    gains = tuple(gains)
    identity = np.eye(count)
    grads = np.concatenate(
        [
            padded(np.kron(derivative, identity), (LANES, LANES)),
            padded(np.kron(identity, derivative), (LANES, LANES)),
        ]
    )
    halves = 2 if kept % 16 == 0 else 1
    order = [list(range(half, kept, halves)) for half in range(halves)]
    flat_order = sum(order, [])
    grad_hi, grad_lo = split_table(grads)
    front_tables = [
        jnp.asarray(np.concatenate([grad_hi, grad_hi, grad_lo], axis=1)),
        jnp.asarray(padded(mass[None], (1, LANES)), jnp.float32),
        jnp.asarray(dft_tables(planes, kept, order)),
    ]

    off_diag = padded(laplace.T - np.diag(lap_diag), (LANES, LANES))
    swap = np.zeros((LANES, LANES))
    for a in range(count):
        swap[a * count, a * count + count - 1] = 1.0
        swap[a * count + count - 1, a * count] = 1.0
    shared = off_diag @ swap
    mat_hi, mat_lo = split_table(np.concatenate([off_diag, shared], axis=1))
    mat = jnp.asarray(np.concatenate([mat_hi, mat_hi, mat_lo], axis=0))
    swap = jnp.asarray(np.concatenate([swap, swap], axis=0), jnp.bfloat16)
    node = np.arange(LANES)
    real = node < nodes
    masks = np.stack(
        [
            real & (node % count == 0),
            real & (node % count == count - 1),
            real & (node // count == 0),
            real & (node // count == count - 1),
        ]
    ).astype(np.float32)
    masks = jnp.asarray(masks)
    lap_row = np.ones((1, LANES))
    lap_row[0, :nodes] = lap_diag
    lap_row = jnp.asarray(lap_row, jnp.float32)
    mass_row = jnp.asarray(padded(mass[None], (1, LANES)), jnp.float32)

    own = penalty.reshape(nodes, local_cols, total_rows).transpose(1, 2, 0)
    own = jnp.pad(own, ((0, 0), (0, 0), (0, LANES - nodes))) * mass_row
    full = jnp.zeros((total_cols, total_rows, LANES), jnp.float32)
    full = lax.dynamic_update_slice(full, own, (spot * local_cols, 0, 0))
    for shift in range(1, owners):
        ring = [(i, (i + shift) % owners) for i in range(owners)]
        other = lax.ppermute(own, "mesh", ring)
        full = lax.dynamic_update_slice(
            full, other, (lax.rem(spot + owners - shift, owners) * local_cols, 0, 0)
        )
    first_row = (lax.axis_index("mode") * owners + spot) * kept
    wave = ((first_row + jnp.asarray(flat_order, jnp.int32)) % MODES).astype(jnp.float32)
    helm = helm_base + (span_wave * wave) ** 2
    wave_mass = helm[:, None] * mass_row

    shape = (groups, owners, local_cols, local_rows)
    total = peers * local * kept
    inverse = pl.pallas_call(
        functools.partial(prep_kernel, shape, count),
        out_shape=pltpu.VMEM((total, LANES), jnp.float32),
        compiler_params=pltpu.CompilerParams(vmem_limit_bytes=GRANT),
        name="prep",
    )(*[resident(v) for v in (wave_mass, full, lap_row, masks)])

    field = velocity.reshape(comps, nodes, local, planes // LANES, LANES)
    field = field.transpose(0, 1, 3, 2, 4).reshape(comps, -1, LANES)

    spot_arg = spot.astype(jnp.int32)[None]
    pieces = {}
    for index, chunk in enumerate(CHUNKS):
        spectra = front(field, chunk, halves, local, front_tables, peers)
        if index:
            spectra, inverse = lax.optimization_barrier((spectra, inverse))
        moved = lax.all_to_all(spectra, ("mode", "mesh"), split_axis=0, concat_axis=0, tiled=True)
        moved = moved.reshape((groups, owners) + moved.shape[1:])
        for slot, component in enumerate(chunk):
            solved = solve(
                shape, midpoint, (count - 1) * count, slot, (0, kept),
                spot_arg, gains, moved, inverse, mat, swap, masks,
            )
            pieces[component, 0] = solved[0]
            for shift in range(1, owners):
                ring = [(i, (i + shift) % owners) for i in range(owners)]
                pieces[component, shift] = lax.ppermute(solved[shift], "mesh", ring)
    shifts = range(1, owners)
    groups_out = [
        [(0, 0), (1, 0)],
        [(2, 0)] + [(c, shift) for c in (0, 1) for shift in shifts],
        [(2, shift) for shift in shifts],
    ]
    result = None
    for group in groups_out:
        if group:
            result = finish(
                [(component, shift, 0) for component, shift in group], owners, kept, flat_order,
                comps, nodes, spot_arg, [pieces[key] for key in group], result,
            )
    result = result[..., :total_rows]
    return result.reshape(kept * owners, comps, count, count, local_cols, total_rows)


def solution(mesh):
    return jax.shard_map(
        step,
        mesh=mesh,
        in_specs=(P(None, None, None, "mesh", "mode", None), P(None, None, "mesh", None)),
        out_specs=P("mode", None, None, None, "mesh", None),
        check_vma=False,
    )
```

```python
import functools
import math

import jax
import jax.numpy as jnp
import numpy as np
from jax import lax
from jax.experimental import pallas as pl
from jax.experimental.pallas import tpu as pltpu
from jax.sharding import PartitionSpec as P

MODES = 256
ITERS = 6
LANES = 128
GRANT = 16 << 20
CHUNKS = ((0, 1), (2,))

helm_base = 1.0
span_wave = 0.02
bound_ratio = 25.0


def legendre_pair(points, order):
    previous = points * 0.0 + 1.0
    current = points * 1.0
    for degree in range(2, order + 1):
        following = ((2 * degree - 1) * points * current - (degree - 1) * previous) / degree
        previous = current
        current = following
    return (current, previous)


def gll_tables(order):
    count = order + 1
    points = -np.cos(np.pi * np.arange(count) / order)
    for _ in range(200):
        top_vals, below_vals = legendre_pair(points, order)
        points = points - (points * top_vals - below_vals) / (count * top_vals)
    legendre_vals, below_vals = legendre_pair(points, order)
    weights = 2.0 / (order * (order + 1) * legendre_vals**2)
    identity = np.eye(count)
    spacing = points[:, None] - points[None, :] + identity
    derivative = legendre_vals[:, None] / (legendre_vals[None, :] * spacing) * (1.0 - identity)
    corner = np.concatenate(
        [[-order * (order + 1) / 4.0], np.zeros(order - 1), [order * (order + 1) / 4.0]]
    )
    derivative = derivative + identity * corner[None, :]
    stiffness = derivative.T @ (weights[:, None] * derivative)
    weight_mat = identity * weights[None, :]
    laplace = np.kron(stiffness, weight_mat) + np.kron(weight_mat, stiffness)
    lap_diag = np.diagonal(laplace)
    upper_bound = float(np.max(np.sum(np.abs(laplace), axis=1) / lap_diag))
    return (weights, derivative, laplace, lap_diag, upper_bound)


def split_table(table):
    table = np.asarray(table, np.float64)
    high = table.astype(jnp.bfloat16)
    low = (table - high.astype(np.float64)).astype(jnp.bfloat16)
    return (high, low)


def split_value(value):
    high = value.astype(jnp.bfloat16)
    low = (value - high.astype(jnp.float32)).astype(jnp.bfloat16)
    return (high, low)


def dft_tables(planes, kept, order):
    halves = len(order)
    first = np.arange(0, 2 * MODES, kept)
    tables = []
    for half in range(halves):
        row = (first[:, None] + np.array(order[half])[None, :]).reshape(-1)
        turns = np.arange(planes // halves)[None, :] * (row % MODES)[:, None] % planes
        angles = 2.0 * np.pi / planes * turns
        table = np.where((row < MODES)[:, None], np.cos(angles), -np.sin(angles))
        high, low = split_table(table / math.sqrt(planes))
        tables.append(np.concatenate([high, low], axis=1))
    return np.stack(tables)


def resident(value):
    return pltpu.with_memory_space_constraint(value, pltpu.VMEM)


def remote(value):
    return pltpu.with_memory_space_constraint(value, pltpu.HBM)


def padded(table, shape):
    result = np.zeros(shape, np.float64)
    result[tuple(slice(0, n) for n in table.shape)] = table
    return result


def dot(a, b, contract=((1,), (0,))):
    return lax.dot_general(a, b, (contract, ((), ())), preferred_element_type=jnp.float32)


def front_kernel(
    chunk, halves, local, field_ref, grad_ref, mass_ref, dft_ref, out_ref, stage, grad, mass, dft, ready, sems, out_sems
):
    comps, flat, lanes = field_ref.shape
    _, _, _, kept_all, rows = out_ref.shape
    kept = kept_all // halves
    planes = dft.shape[2] // 2 * halves
    pieces = planes // lanes
    nodes = flat // (pieces * local)
    order = [0, 1] + [c for c in chunk if c > 1]
    copies = {c: pltpu.make_async_copy(field_ref.at[c], stage.at[c], sems.at[c]) for c in order}
    grad_copy = pltpu.make_async_copy(grad_ref, grad, sems.at[comps])
    dft_copy = pltpu.make_async_copy(dft_ref, dft, sems.at[comps + 1])
    mass_copy = pltpu.make_async_copy(mass_ref, mass, sems.at[comps + 2])
    copies[0].start()
    grad_copy.start()
    for c in order[1:]:
        copies[c].start()
    dft_copy.start()
    mass_copy.start()
    gap = jnp.zeros((rows - nodes, planes), jnp.float32)

    def read(c, e):
        parts = [
            stage[c, pl.ds(piece * local + e, nodes, stride=pieces * local), :]
            for piece in range(pieces)
        ]
        return jnp.concatenate([jnp.concatenate(parts, axis=1), gap], axis=0)

    grad_copy.wait()
    copies[0].wait()
    copies[1].wait()
    for c in order[2:]:
        copies[c].wait()
    sent = []
    for slot, c in enumerate(chunk):
        for start in range(0, local, 2):
            elements = range(start, min(start + 2, local))
            folded = [[] for _ in range(halves)]
            for e in elements:
                value = read(c, e)
                high, low = split_value(value)
                slope = dot(grad[...], jnp.concatenate([high, low, high], axis=0))
                forcing = value - (read(0, e) * slope[:rows] + read(1, e) * slope[rows:])
                if halves == 2:
                    near, far = forcing[:, : planes // 2], forcing[:, planes // 2 :]
                    folded[0].append(near + far)
                    folded[1].append(near - far)
                else:
                    folded[0].append(forcing)
            if slot == 0 and start == 0:
                dft_copy.wait()
                mass_copy.wait()
            for half in range(halves):
                high, low = split_value(jnp.concatenate(folded[half], axis=0))
                table = dft[half]
                spectra = dot(
                    jnp.concatenate([table[:, : planes // halves], table], axis=1),
                    jnp.concatenate([high, low, high], axis=1),
                    ((1,), (1,)),
                )
                for i, e in enumerate(elements):
                    part = spectra[:, i * rows : (i + 1) * rows] * mass[...]
                    ready[:, slot, e, half * kept : (half + 1) * kept, :] = part.reshape(
                        out_ref.shape[0], kept, rows
                    )
        copy = pltpu.make_async_copy(ready.at[:, slot], out_ref.at[:, slot], out_sems.at[slot])
        copy.start()
        sent.append(copy)
    for copy in sent:
        copy.wait()


def front(field, chunk, halves, local, tables, peers):
    grad, mass, dft = tables
    kept = dft.shape[0] * dft.shape[1] // peers
    far = pl.BlockSpec(memory_space=pltpu.HBM)
    shape = (peers, len(chunk), local, kept, LANES)
    return pl.pallas_call(
        functools.partial(front_kernel, chunk, halves, local),
        out_shape=pltpu.HBM(shape, jnp.float32),
        in_specs=[far] * 4,
        out_specs=far,
        scratch_shapes=[
            pltpu.VMEM(field.shape, jnp.float32),
            pltpu.VMEM(grad.shape, grad.dtype),
            pltpu.VMEM(mass.shape, mass.dtype),
            pltpu.VMEM(dft.shape, dft.dtype),
            pltpu.VMEM(shape, jnp.float32),
            pltpu.SemaphoreType.DMA((field.shape[0] + 3,)),
            pltpu.SemaphoreType.DMA((len(chunk),)),
        ],
        compiler_params=pltpu.CompilerParams(vmem_limit_bytes=GRANT),
    )(*[remote(value) for value in (field, grad, mass, dft)])


def side_sum(value, before, after, masks):
    first, last = masks
    extra = 0.0
    if before is not None:
        extra = jnp.where(first, before, extra)
    if after is not None:
        extra = jnp.where(last, after, extra)
    return value if before is None and after is None else value + extra


def across(line, masks, side):
    result = []
    for col, value in enumerate(line):
        before = pltpu.roll(line[col - 1], LANES - side, 1) if col > 0 else None
        after = pltpu.roll(line[col + 1], side, 1) if col + 1 < len(line) else None
        result.append(side_sum(value, before, after, masks))
    return result


def read_masks(mask_ref, kept):
    bottom, top, left, right = (
        jnp.broadcast_to(mask_ref[i : i + 1, :], (kept, LANES)) > 0.5 for i in range(4)
    )
    return (bottom, top), (left, right)


def places(shape, kept):
    groups, owners, local_cols, local_rows = shape
    table = []
    for col in range(owners * local_cols):
        owner, lc = divmod(col, local_cols)
        line = []
        for row in range(groups * local_rows):
            part, e = divmod(row, local_rows)
            line.append((((part * owners + owner) * local_cols + lc) * local_rows + e) * kept)
        table.append(line)
    return table


def prep_kernel(shape, count, wave_ref, pen_ref, lap_ref, mask_ref, inverse_ref):
    kept = wave_ref.shape[0]
    along, over = read_masks(mask_ref, kept)
    where = places(shape, kept)
    cols, rows = len(where), len(where[0])
    base = wave_ref[...] + lap_ref[...]
    edge = pltpu.roll(base, count - 1, 1), pltpu.roll(base, LANES - count + 1, 1)
    for row in range(rows):
        line = []
        for col in range(cols):
            before = after = None
            if row > 0:
                other = pltpu.roll(pen_ref[col, row - 1 : row, :], LANES - count + 1, 1)
                before = edge[1] + other
            if row + 1 < rows:
                after = edge[0] + pltpu.roll(pen_ref[col, row + 1 : row + 2, :], count - 1, 1)
            line.append(side_sum(base + pen_ref[col, row : row + 1, :], before, after, along))
        for col, value in enumerate(across(line, over, (count - 1) * count)):
            first = where[col][row]
            inverse_ref[first : first + kept, :] = 1.0 / value


def solve_kernel(
    shape, midpoint, side, slot, span, gains, spot_ref, src_ref, inverse_ref, mat_ref, swap_ref, mask_ref, *rest
):
    groups, owners, local_cols, local_rows = shape
    outs = rest[:-5]
    work_ref, edge_ref, res_ref, dir_ref, sum_ref = rest[-5:]
    begin, end = span
    kept = end - begin
    along, over = read_masks(mask_ref, kept)
    where = places(shape, kept)
    whole = places(shape, src_ref.shape[-2])
    cols, rows_all = len(where), len(where[0])
    total = cols * rows_all * kept
    steps = math.gcd(groups, 2)
    block = total // steps
    parts = groups // steps

    def assembled(main, row):
        line = []
        for col in range(cols):
            before = after = None
            if row > 0:
                before = edge_ref[pl.ds(where[col][row - 1], kept), :]
            if row + 1 < rows_all:
                after = edge_ref[pl.ds(where[col][row + 1], kept), :]
            line.append(side_sum(main(col, row), before, after, along))
        return across(line, over, side)

    def source(col, row):
        owner, lc = divmod(col, local_cols)
        part, e = divmod(row, local_rows)
        return src_ref[part, owner, slot, lc * local_rows + e, begin:end]

    def inverse(col, row):
        return inverse_ref[pl.ds(whole[col][row] + begin, kept), :]

    def work(col, row):
        return work_ref[pl.ds(where[col][row], kept), :]

    for step in range(steps):
        values = src_ref[step * parts : (step + 1) * parts, :, slot, :, begin:end]
        values = values.reshape(block, LANES)
        high, low = split_value(values)
        edge_ref[pl.ds(step * block, block), :] = dot(
            jnp.concatenate([high, low], axis=1), swap_ref[...]
        )
    for row in range(rows_all):
        for col, value in enumerate(assembled(source, row)):
            here = pl.ds(where[col][row], kept)
            residual = inverse(col, row) * value
            direction = residual * (1.0 / midpoint)
            res_ref[here, :] = residual
            dir_ref[here, :] = direction
            sum_ref[pl.ds((col * rows_all + row) * kept, kept), :] = direction

    def sweep(step, carry):
        keep, gain = (jnp.float32(value) for value in gains[0])
        for i, (next_keep, next_gain) in enumerate(gains[1:]):
            keep = jnp.where(step > i, jnp.float32(next_keep), keep)
            gain = jnp.where(step > i, jnp.float32(next_gain), gain)

        def multiply(start):
            high, low = split_value(dir_ref[pl.ds(start, block), :])
            product = dot(jnp.concatenate([high, low, high], axis=1), mat_ref[...])
            work_ref[pl.ds(start, block), :] = product[:, :LANES]
            edge_ref[pl.ds(start, block), :] = product[:, LANES:]

        def update(row):
            for col, value in enumerate(assembled(work, row)):
                here = pl.ds(where[col][row], kept)
                direction = dir_ref[here, :]
                residual = res_ref[here, :] - direction - inverse(col, row) * value
                direction = keep * direction + gain * residual
                res_ref[here, :] = residual
                dir_ref[here, :] = direction
                there = pl.ds((col * rows_all + row) * kept, kept)
                sum_ref[there, :] = sum_ref[there, :] + direction

        done = 0
        multiply(0)
        for piece in range(1, steps + 1):
            if piece < steps:
                multiply(piece * block)
            ready = rows_all if piece == steps else piece * parts * local_rows - 1
            for row in range(done, ready):
                update(row)
            done = ready
        return carry

    lax.fori_loop(0, ITERS - 1, sweep, 0)

    spot = spot_ref[0]
    for shift, out in enumerate(outs):
        for lc in range(local_cols):
            col = lax.rem(spot + shift, owners) * local_cols + lc
            for k in range(kept):
                out[k, lc] = sum_ref[pl.ds(col * (rows_all * kept) + k, rows_all, stride=kept), :]


def solve(shape, midpoint, side, slot, span, spot, gains, moved, inverse, mat, swap, masks):
    groups, owners, local_cols, local_rows = shape
    kept = span[1] - span[0]
    rows = groups * local_rows
    total = owners * local_cols * rows * kept
    piece = pltpu.VMEM((kept, local_cols, rows, LANES), jnp.float32)
    smem = pl.BlockSpec(memory_space=pltpu.SMEM)
    vmem = pl.BlockSpec(memory_space=pltpu.VMEM)
    return pl.pallas_call(
        functools.partial(solve_kernel, shape, midpoint, side, slot, span, gains),
        out_shape=[piece] * owners,
        in_specs=[
            smem,
            vmem,
            vmem,
            vmem,
            vmem,
            vmem,
        ],
        out_specs=[vmem] * owners,
        scratch_shapes=[pltpu.VMEM((total, LANES), jnp.float32)] * 5,
        compiler_params=pltpu.CompilerParams(vmem_limit_bytes=GRANT),
    )(spot, *[resident(v) for v in (moved, inverse, mat, swap, masks)])


def finish_kernel(parts, owners, kept, order, spot_ref, *rest):
    sources = rest[: len(parts)]
    out_ref, stage_ref, sems = rest[-3:]
    nodes, local_cols, lanes = out_ref.shape[2:]
    rows = sources[0].shape[2]
    fit = lanes // rows
    copies = []
    for source, (component, shift, begin) in zip(sources, parts):
        place = lax.rem(spot_ref[0] + (owners - shift), owners) * kept
        count = source.shape[0]
        for first in range(0, count, fit):
            group = range(first, min(first + fit, count))
            for lc in range(local_cols):
                block = [source[k, lc] for k in group]
                if len(group) * rows < lanes:
                    block.append(jnp.zeros((lanes - len(group) * rows, LANES), jnp.float32))
                turned = jnp.concatenate(block, axis=0).T
                for i, k in enumerate(group):
                    value = pltpu.roll(turned, lanes - i * rows, 1) if i else turned
                    index = len(copies)
                    stage_ref[pl.ds(index * LANES, LANES), :] = value
                    target = out_ref.at[place + order[begin + k], component, :, lc, :]
                    held = stage_ref.at[pl.ds(index * LANES, nodes)]
                    copy = pltpu.make_async_copy(held, target, sems.at[index])
                    copy.start()
                    copies.append(copy)
    for copy in copies:
        copy.wait()


def finish(parts, owners, kept, order, comps, nodes, spot, sources, so_far):
    _, local_cols, rows, _ = sources[0].shape
    width = pl.cdiv(rows, LANES) * LANES
    count = sum(source.shape[0] for source in sources) * local_cols
    keep_out = pl.BlockSpec(memory_space=pl.ANY)
    in_specs = [pl.BlockSpec(memory_space=pltpu.SMEM)]
    in_specs += [pl.BlockSpec(memory_space=pltpu.VMEM)] * len(sources)
    args = [spot] + [resident(source) for source in sources]
    aliases = {}
    if so_far is not None:
        aliases = {len(args): 0}
        in_specs.append(keep_out)
        args.append(so_far)
    return pl.pallas_call(
        functools.partial(finish_kernel, parts, owners, kept, order),
        out_shape=jax.ShapeDtypeStruct((kept * owners, comps, nodes, local_cols, width), jnp.float32),
        in_specs=in_specs,
        out_specs=keep_out,
        scratch_shapes=[
            pltpu.VMEM((count * LANES, width), jnp.float32),
            pltpu.SemaphoreType.DMA((count,)),
        ],
        input_output_aliases=aliases,
        compiler_params=pltpu.CompilerParams(vmem_limit_bytes=GRANT),
    )(*args)


def step(velocity, penalty):
    comps, count, _, local_cols, local_rows, planes = velocity.shape
    nodes = count * count
    groups = lax.axis_size("mode")
    owners = lax.axis_size("mesh")
    peers = groups * owners
    spot = lax.axis_index("mesh")
    local = local_cols * local_rows
    kept = 2 * MODES // peers
    total_cols = owners * local_cols
    total_rows = groups * local_rows

    weights, derivative, laplace, lap_diag, upper_bound = gll_tables(count - 1)
    mass = np.kron(weights, weights)
    lower_bound = upper_bound / bound_ratio
    midpoint = (upper_bound + lower_bound) / 2.0
    half_width = (upper_bound - lower_bound) / 2.0
    recurrence = half_width / midpoint
    gains = []
    for _ in range(1, ITERS):
        following = 1.0 / (2.0 * midpoint / half_width - recurrence)
        gains.append((following * recurrence, 2.0 * following / half_width))
        recurrence = following
    gains = tuple(gains)
    identity = np.eye(count)
    grads = np.concatenate(
        [
            padded(np.kron(derivative, identity), (LANES, LANES)),
            padded(np.kron(identity, derivative), (LANES, LANES)),
        ]
    )
    halves = 2 if kept % 16 == 0 else 1
    order = [list(range(half, kept, halves)) for half in range(halves)]
    flat_order = sum(order, [])
    grad_hi, grad_lo = split_table(grads)
    front_tables = [
        jnp.asarray(np.concatenate([grad_hi, grad_hi, grad_lo], axis=1)),
        jnp.asarray(padded(mass[None], (1, LANES)), jnp.float32),
        jnp.asarray(dft_tables(planes, kept, order)),
    ]

    off_diag = padded(laplace.T - np.diag(lap_diag), (LANES, LANES))
    swap = np.zeros((LANES, LANES))
    for a in range(count):
        swap[a * count, a * count + count - 1] = 1.0
        swap[a * count + count - 1, a * count] = 1.0
    shared = off_diag @ swap
    mat_hi, mat_lo = split_table(np.concatenate([off_diag, shared], axis=1))
    mat = jnp.asarray(np.concatenate([mat_hi, mat_hi, mat_lo], axis=0))
    swap = jnp.asarray(np.concatenate([swap, swap], axis=0), jnp.bfloat16)
    node = np.arange(LANES)
    real = node < nodes
    masks = np.stack(
        [
            real & (node % count == 0),
            real & (node % count == count - 1),
            real & (node // count == 0),
            real & (node // count == count - 1),
        ]
    ).astype(np.float32)
    masks = jnp.asarray(masks)
    lap_row = np.ones((1, LANES))
    lap_row[0, :nodes] = lap_diag
    lap_row = jnp.asarray(lap_row, jnp.float32)
    mass_row = jnp.asarray(padded(mass[None], (1, LANES)), jnp.float32)

    own = penalty.reshape(nodes, local_cols, total_rows).transpose(1, 2, 0)
    own = jnp.pad(own, ((0, 0), (0, 0), (0, LANES - nodes))) * mass_row
    full = jnp.zeros((total_cols, total_rows, LANES), jnp.float32)
    full = lax.dynamic_update_slice(full, own, (spot * local_cols, 0, 0))
    for shift in range(1, owners):
        ring = [(i, (i + shift) % owners) for i in range(owners)]
        other = lax.ppermute(own, "mesh", ring)
        full = lax.dynamic_update_slice(
            full, other, (lax.rem(spot + owners - shift, owners) * local_cols, 0, 0)
        )
    first_row = (lax.axis_index("mode") * owners + spot) * kept
    wave = ((first_row + jnp.asarray(flat_order, jnp.int32)) % MODES).astype(jnp.float32)
    helm = helm_base + (span_wave * wave) ** 2
    wave_mass = helm[:, None] * mass_row

    shape = (groups, owners, local_cols, local_rows)
    total = peers * local * kept
    inverse = pl.pallas_call(
        functools.partial(prep_kernel, shape, count),
        out_shape=pltpu.VMEM((total, LANES), jnp.float32),
        compiler_params=pltpu.CompilerParams(vmem_limit_bytes=GRANT),
        name="prep",
    )(*[resident(v) for v in (wave_mass, full, lap_row, masks)])

    field = velocity.reshape(comps, nodes, local, planes // LANES, LANES)
    field = field.transpose(0, 1, 3, 2, 4).reshape(comps, -1, LANES)

    spot_arg = spot.astype(jnp.int32)[None]
    pieces = {}
    for index, chunk in enumerate(CHUNKS):
        spectra = front(field, chunk, halves, local, front_tables, peers)
        if index:
            spectra, inverse = lax.optimization_barrier((spectra, inverse))
        moved = lax.all_to_all(spectra, ("mode", "mesh"), split_axis=0, concat_axis=0, tiled=True)
        moved = moved.reshape((groups, owners) + moved.shape[1:])
        for slot, component in enumerate(chunk):
            final = component == CHUNKS[-1][-1]
            width = kept // halves if final else kept
            for begin in range(0, kept, width):
                solved = solve(
                    shape, midpoint, (count - 1) * count, slot, (begin, begin + width),
                    spot_arg, gains, moved, inverse, mat, swap, masks,
                )
                pieces[component, 0, begin] = solved[0]
                for shift in range(1, owners):
                    ring = [(i, (i + shift) % owners) for i in range(owners)]
                    pieces[component, shift, begin] = lax.ppermute(solved[shift], "mesh", ring)
    shifts = range(1, owners)
    begins = range(0, kept, kept // halves)
    groups_out = [
        [(0, 0, 0), (1, 0, 0)],
        [(2, 0, begin) for begin in begins] + [(c, shift, 0) for c in (0, 1) for shift in shifts],
    ]
    groups_out += [[(2, shift, begin) for shift in shifts] for begin in begins]
    result = None
    for group in groups_out:
        if group:
            result = finish(
                group, owners, kept, flat_order,
                comps, nodes, spot_arg, [pieces[key] for key in group], result,
            )
    result = result[..., :total_rows]
    return result.reshape(kept * owners, comps, count, count, local_cols, total_rows)


def solution(mesh):
    return jax.shard_map(
        step,
        mesh=mesh,
        in_specs=(P(None, None, None, "mesh", "mode", None), P(None, None, "mesh", None)),
        out_specs=P("mode", None, None, None, "mesh", None),
        check_vma=False,
    )
```
